32 devices in a mesh: space: 8 (over z, y), band: 4 (over x, core).
Axes of the slice: x: 2, y: 2, z: 4, core: 2. Of those that a mesh axis runs over, the one named last changes fastest.
Arguments:
- columns: float32 [16, 48, 32, 128], P('band', 'space'), may hold values from -6 to 6
- potential: float32 [48, 32, 128], P('space'), may hold values from -1 to 3
- orbitals: float32 [512, 48, 32, 128], P('band', 'space'), may hold values from -0.0546875 to 0.0546875
Outputs:
- projected: float32 [16, 48, 32, 128], P('band', 'space')
- correlation: float32 [512, 16], P('band')
The draws below stay inside these ranges and needn't reach their ends.
All inputs are finite; a program needn't handle non-finite values.
Results may differ from the reference program's by a relative error of at most 0.00011.
Values sent between devices are 32-bit elements; how exact they have to be, the bound alone decides.
No kernel may reach another device: no remote copies, remote signals or barrier semaphores. Data moves between devices by JAX's collectives and lax.ppermute only.
A program may use at most 128 MiB of HBM per device.

```python
import jax
import jax.numpy as jnp
from jax import lax

NY = 32
NX = 128
ORBS = 512
NZ = 48
COLS = 16


def steps_of(key, dims, cuts, low, high):
    factor_of = 1.0
    for axis_at, blocks in cuts:
        heights = jax.random.uniform(jax.random.fold_in(jax.random.fold_in(key, 6), axis_at), (blocks,), jnp.float32, low / len(cuts), high / len(cuts))
        factor_of = factor_of * jnp.repeat(jnp.exp(heights), dims[axis_at] // blocks).reshape((-1,) + (1,) * (len(dims) - 1 - axis_at))
    return factor_of


def centred(own_key, shape, deviation, limit, split=(), kind=jnp.bfloat16):
    level = steps_of(own_key, shape, split, -0.22, 0.18) if split else 1.0
    values = jax.random.normal(own_key, shape, jnp.float32) * deviation * level
    return jnp.minimum(jnp.maximum(values, -limit), limit).astype(kind)


def setup_inputs(seed: int = 0) -> dict:
    keys = jax.random.split(jax.random.key(seed), 4)
    return {
        "columns": centred(keys[0], (COLS, NZ, NY, NX), 1.0, 6.0, ((0, 4), (1, 8)), jnp.float32),
        "potential": jnp.clip(-1.0 + 4.0 * jax.random.uniform(keys[1], (NZ, NY, NX), jnp.float32) ** steps_of(keys[1], (NZ, NY, NX), ((0, 8),), -0.2, 0.2), -1.0, 3.0),
        "orbitals": centred(keys[2], (ORBS, NZ, NY, NX), (NZ * NY * NX // 16) ** -0.5, 0.0546875, ((0, 4), (1, 8)), jnp.float32),
    }


COEFFS = (-5369.0 / 1800.0, 12.0 / 7.0, -15.0 / 56.0, 10.0 / 189.0, -1.0 / 112.0, 2.0 / 1925.0, -1.0 / 16632.0)


def hamiltonian(values, potential):
    laplace = 3.0 * COEFFS[0] * values
    for offset in range(1, 7):
        along = jnp.roll(values, offset, 1) + jnp.roll(values, -offset, 1)
        along = along + jnp.roll(values, offset, 2) + jnp.roll(values, -offset, 2)
        along = along + jnp.roll(values, offset, 3) + jnp.roll(values, -offset, 3)
        laplace = laplace + COEFFS[offset] * along
    return -0.5 * laplace + potential[None] * values


def reference(columns, potential, orbitals):
    applied = hamiltonian(columns, potential)
    psi_flat = orbitals.reshape(orbitals.shape[0], -1)
    applied_flat = applied.reshape(applied.shape[0], -1)
    correlation = jnp.einsum("oc,kc->ok", psi_flat, applied_flat, precision=lax.Precision.HIGHEST)
    removed = jnp.einsum("ok,oc->kc", correlation, psi_flat, precision=lax.Precision.HIGHEST)
    projected = (applied_flat - removed).reshape(applied.shape)
    return projected, correlation
```

```python
import functools

import jax
import jax.numpy as jnp
from jax import lax
from jax.experimental import pallas as pl
from jax.experimental.pallas import tpu as pltpu
from jax.sharding import PartitionSpec as P

COEFFS = (
    -5369.0 / 1800.0,
    12.0 / 7.0,
    -15.0 / 56.0,
    10.0 / 189.0,
    -1.0 / 112.0,
    2.0 / 1925.0,
    -1.0 / 16632.0,
)
WIDTH = 6
SUB = 8
F32 = jnp.float32
BF16 = jnp.bfloat16
VMEM = pl.BlockSpec(memory_space=pltpu.VMEM)
LIMIT = 24 << 20


def near(x):
    return pltpu.with_memory_space_constraint(x, pltpu.VMEM)


def params(limit=LIMIT):
    return pltpu.CompilerParams(vmem_limit_bytes=limit)


def halves(x):
    hi = x.astype(BF16)
    lo = (x - hi.astype(F32)).astype(BF16)
    return hi, lo


def split_kernel(psi_ref, hi_ref, lo_ref):
    orbs = psi_ref.shape[0]
    lanes = psi_ref.shape[3]
    for g in range(psi_ref.shape[2] // SUB):
        x = psi_ref[:, 0, g * SUB : (g + 1) * SUB, :].reshape(orbs * SUB, lanes)
        hi, lo = halves(x)
        hi_ref[pl.program_id(0), :, g * lanes : (g + 1) * lanes] = hi
        lo_ref[pl.program_id(0), :, g * lanes : (g + 1) * lanes] = lo


def split(orbitals):
    orbs, planes, ny, nx = orbitals.shape
    rows = 2 * SUB
    per = ny // rows
    shape = pltpu.VMEM((planes * per, orbs * SUB, 2 * nx), BF16)
    return pl.pallas_call(
        split_kernel,
        grid=(planes * per,),
        in_specs=[pl.BlockSpec((orbs, 1, rows, nx), lambda p: (0, p // per, p % per, 0))],
        out_specs=[VMEM, VMEM],
        out_shape=[shape, shape],
        compiler_params=params(),
        cost_estimate=pl.CostEstimate(
            flops=4 * orbitals.size, bytes_accessed=8 * orbitals.size, transcendentals=0
        ),
        name="split",
    )(orbitals)


def local_kernel(v_ref, pot_ref, out_ref):
    cols, planes, _, _ = v_ref.shape

    def column(c, carry):
        for z in range(planes):
            v = v_ref[c, z]
            total = (pot_ref[z] - 1.5 * COEFFS[0]) * v
            for k in range(1, WIDTH + 1):
                along = pltpu.roll(v, k, 1) + pltpu.roll(v, v.shape[1] - k, 1)
                along = along + pltpu.roll(v, k, 0) + pltpu.roll(v, v.shape[0] - k, 0)
                if z + k < planes:
                    along = along + v_ref[c, z + k]
                if z - k >= 0:
                    along = along + v_ref[c, z - k]
                total = total - (0.5 * COEFFS[k]) * along
            out_ref[c, z] = total
        return carry

    lax.fori_loop(0, cols, column, 0)


def halo_kernel(own_ref, before_ref, after_ref, out_ref):
    cols, planes, _, _ = own_ref.shape

    def column(c, carry):
        for z in range(planes):
            total = own_ref[c, z]
            for k in range(1, WIDTH + 1):
                if z - k < 0:
                    total = total - (0.5 * COEFFS[k]) * before_ref[c, WIDTH + z - k]
                if z + k >= planes:
                    total = total - (0.5 * COEFFS[k]) * after_ref[c, z + k - planes]
            out_ref[c, z] = total
        return carry

    lax.fori_loop(0, cols, column, 0)


def rows_of(refs, z, y):
    return jnp.concatenate(
        [
            jnp.concatenate(
                [
                    ref[:, z, y + g * SUB : y + (g + 1) * SUB, :].reshape(
                        ref.shape[0] * SUB, ref.shape[3]
                    )
                    for ref in refs
                ],
                axis=0,
            )
            for g in range(2)
        ],
        axis=1,
    )


def corr_kernel(count, hi_ref, lo_ref, *refs):
    blocks, out_ref = refs[:count], refs[count]
    big_ref, small_ref = refs[count + 1 :]
    pairs, rows, _ = hi_ref.shape
    planes, ny = blocks[0].shape[1:3]
    per = ny // (2 * SUB)
    width = sum(b.shape[0] for b in blocks) * SUB
    contract = (((1,), (1,)), ((), ()))
    for p in range(pairs):
        w_hi, w_lo = halves(rows_of(blocks, p // per, (p % per) * 2 * SUB))
        both = jnp.concatenate([w_hi, w_lo], axis=0)
        big = lax.dot_general(hi_ref[p], both, contract, preferred_element_type=F32)
        small = lax.dot_general(lo_ref[p], w_hi, contract, preferred_element_type=F32)
        if p == 0:
            big_ref[...] = big
            small_ref[...] = small
        else:
            big_ref[...] += big
            small_ref[...] += small
    total = big_ref[:, :width] + big_ref[:, width:] + small_ref[...]
    total = total.reshape(rows // SUB, SUB, width)
    at = lax.broadcasted_iota(jnp.int32, total.shape, 1)
    lane = lax.broadcasted_iota(jnp.int32, total.shape, 2)
    diag = jnp.sum(jnp.where(lane % SUB == at, total, 0.0), axis=1)
    cols = width // SUB
    pick = lax.broadcasted_iota(jnp.int32, (cols, width), 1) // SUB
    pick = pick == lax.broadcasted_iota(jnp.int32, (cols, width), 0)
    out_ref[...] = lax.dot_general(
        pick.astype(F32),
        diag,
        contract,
        precision=lax.Precision.HIGHEST,
        preferred_element_type=F32,
    )


def correlate(hi, lo, blocks):
    cols = sum(b.shape[0] for b in blocks)
    orbs = hi.shape[1] // SUB
    return pl.pallas_call(
        functools.partial(corr_kernel, len(blocks)),
        in_specs=[VMEM] * (2 + len(blocks)),
        out_specs=VMEM,
        out_shape=pltpu.VMEM((cols, orbs), F32),
        compiler_params=params(),
        scratch_shapes=[
            pltpu.VMEM((orbs * SUB, 2 * cols * SUB), F32),
            pltpu.VMEM((orbs * SUB, cols * SUB), F32),
        ],
        name="corr",
    )(near(hi), near(lo), *map(near, blocks))


def add_kernel(*refs):
    total = refs[0][...]
    for ref in refs[1:-1]:
        total = total + ref[...]
    refs[-1][...] = total


def add(*parts):
    return pl.pallas_call(
        add_kernel,
        in_specs=[VMEM] * len(parts),
        out_specs=VMEM,
        out_shape=pltpu.VMEM(parts[0].shape, F32),
        compiler_params=params(),
        name="add",
    )(*map(near, parts))


def remove_kernel(order, count, me_ref, *refs):
    parts = refs[:count]
    hi_ref, lo_ref, out_ref, keep_ref, send_ref = refs[count:]
    cols, orbs = out_ref.shape
    pairs, rows, wide = hi_ref.shape
    nx = wide // 2
    per = keep_ref.shape[2] // (2 * SUB)
    half = keep_ref.shape[0]
    corr = parts[0][...]
    for part in parts[1:]:
        corr = corr + part[...]
    step = cols // len(order)
    pieces = [None] * len(order)
    for at, r in enumerate(order):
        pieces[r] = corr[at * step : (at + 1) * step]
    mask = 1
    while mask < len(order):
        swap = (me_ref[0] & mask) != 0
        pieces = [jnp.where(swap, pieces[r ^ mask], pieces[r]) for r in range(len(order))]
        mask *= 2
    out_ref[...] = jnp.concatenate(pieces, axis=0)

    spread = lax.broadcasted_iota(jnp.int32, (orbs, rows), 1) // SUB
    spread = (spread == lax.broadcasted_iota(jnp.int32, (orbs, rows), 0)).astype(BF16)
    tall = jnp.broadcast_to(corr[:, None, :], (cols, SUB, orbs)).reshape(cols * SUB, orbs)
    at = lax.broadcasted_iota(jnp.int32, (cols * SUB, rows), 0) % SUB
    same = at == lax.broadcasted_iota(jnp.int32, (cols * SUB, rows), 1) % SUB
    c_hi, c_lo = [
        jnp.where(same, jnp.dot(part, spread, preferred_element_type=F32), 0.0).astype(BF16)
        for part in halves(tall)
    ]
    both = jnp.concatenate([c_hi, c_lo], axis=0)
    height = cols * SUB
    for p in range(pairs):
        big = jnp.dot(both, hi_ref[p], preferred_element_type=F32)
        small = jnp.dot(c_hi, lo_ref[p], preferred_element_type=F32)
        total = big[:height] + big[height:] + small
        z, y = p // per, (p % per) * 2 * SUB
        for g in range(2):
            part = total[:, g * nx : (g + 1) * nx].reshape(cols, SUB, nx)
            keep_ref[:, z, y + g * SUB : y + (g + 1) * SUB, :] = part[:half]
            send_ref[:, z, y + g * SUB : y + (g + 1) * SUB, :] = part[half:]


def remove(order, me, parts, hi, lo, planes, ny, nx):
    cols, orbs = parts[0].shape
    part = pltpu.VMEM((cols // 2, planes, ny, nx), F32)
    return pl.pallas_call(
        functools.partial(remove_kernel, order, len(parts)),
        in_specs=[pl.BlockSpec(memory_space=pltpu.SMEM)] + [VMEM] * (len(parts) + 2),
        out_specs=[VMEM] * 3,
        out_shape=[pltpu.VMEM((cols, orbs), F32), part, part],
        compiler_params=params(),
        name="remove",
    )(me, *map(near, parts), near(hi), near(lo))


def swap(x, axis, mask):
    size = lax.axis_size(axis)
    return lax.ppermute(x, axis, [(i, i ^ mask) for i in range(size)])


def shards(columns, potential, orbitals):
    cols, planes, ny, nx = columns.shape
    space, band = lax.axis_size("space"), lax.axis_size("band")
    up = [(i, (i + 1) % space) for i in range(space)]
    down = [(j, i) for i, j in up]
    before = lax.ppermute(columns[:, planes - WIDTH :], "space", up)
    after = lax.ppermute(columns[:, :WIDTH], "space", down)
    me = lax.axis_index("band").astype(jnp.int32).reshape(1)
    orbitals, me = lax.optimization_barrier((orbitals, me))
    hi, lo = split(orbitals)
    shape = pltpu.VMEM(columns.shape, F32)
    own = pl.pallas_call(
        local_kernel,
        in_specs=[VMEM] * 2,
        out_specs=VMEM,
        out_shape=shape,
        compiler_params=params(),
        name="local",
    )(near(columns), near(potential))
    own, hi, lo = lax.optimization_barrier((own, hi, lo))
    applied = pl.pallas_call(
        halo_kernel,
        in_specs=[VMEM] * 3,
        out_specs=VMEM,
        out_shape=shape,
        compiler_params=params(),
        name="halo",
    )(near(own), near(before), near(after))

    blocks, order = [applied], [0]
    mask = band // 2
    while mask:
        blocks = blocks + [swap(block, "band", mask) for block in blocks]
        order = order + [r ^ mask for r in order]
        mask //= 2
    corr = correlate(hi, lo, blocks)
    steps = [[1, 2, 3]] + [[1 << bit] for bit in range(2, space.bit_length() - 1)]
    parts = [corr]
    for step in steps:
        held = parts[0] if len(parts) == 1 else add(*parts)
        parts = [held] + [swap(held, "space", mask) for mask in step]
    corr, keep, send = remove(order, me, parts, hi, lo, planes, ny, nx)
    mask = 1
    while mask < band:
        kept = keep + swap(send, "band", mask)
        half = kept.shape[0] // 2
        keep, send = kept[:half], kept[half:]
        mask *= 2
    return applied - kept, corr.T


def solution(mesh):
    placed = (
        P("band", "space", None, None),
        P("space", None, None),
        P("band", "space", None, None),
    )
    return jax.shard_map(
        shards,
        mesh=mesh,
        in_specs=placed,
        out_specs=(P("band", "space", None, None), P("band", None)),
        check_vma=False,
    )
```

```python
import functools

import jax
import jax.numpy as jnp
from jax import lax
from jax.experimental import pallas as pl
from jax.experimental.pallas import tpu as pltpu
from jax.sharding import PartitionSpec as P

COEFFS = (
    -5369.0 / 1800.0,
    12.0 / 7.0,
    -15.0 / 56.0,
    10.0 / 189.0,
    -1.0 / 112.0,
    2.0 / 1925.0,
    -1.0 / 16632.0,
)
WIDTH = 6
SUB = 8
F32 = jnp.float32
BF16 = jnp.bfloat16
VMEM = pl.BlockSpec(memory_space=pltpu.VMEM)
LIMIT = 16 << 20


def near(x):
    return pltpu.with_memory_space_constraint(x, pltpu.VMEM)


def far_off(x):
    return pltpu.with_memory_space_constraint(x, pltpu.HBM)


def params(limit=LIMIT):
    return pltpu.CompilerParams(vmem_limit_bytes=limit)


def halves(x):
    hi = x.astype(BF16)
    lo = (x - hi.astype(F32)).astype(BF16)
    return hi, lo


def cut_kernel(cuts, columns_ref, pot_ref, *refs):
    outs, sems = refs[:-1], refs[-1]
    copies = [pltpu.make_async_copy(pot_ref, outs[-1], sems.at[len(cuts)])]
    copies[0].start()
    for at, (a, b) in enumerate(cuts):
        source = columns_ref.at[pl.ds(a, b - a)]
        copies.append(pltpu.make_async_copy(source, outs[at], sems.at[at]))
        copies[-1].start()
    for copy in copies:
        copy.wait()


def cut(columns, potential, cuts):
    shapes = [(b - a,) + columns.shape[1:] for a, b in cuts] + [potential.shape]
    return pl.pallas_call(
        functools.partial(cut_kernel, cuts),
        in_specs=[pl.BlockSpec(memory_space=pl.ANY)] * 2,
        out_specs=[VMEM] * len(shapes),
        out_shape=[pltpu.VMEM(shape, F32) for shape in shapes],
        scratch_shapes=[pltpu.SemaphoreType.DMA((len(shapes),))],
        compiler_params=params(),
        name="cut",
    )(far_off(columns), far_off(potential))


def split_kernel(first, count, psi_ref, hi_ref, lo_ref, held_ref, sems):
    orbs, planes, ny, lanes = held_ref.shape
    per = ny // (2 * SUB)
    block = orbs // count
    copies = []
    for at in range(count):
        source = psi_ref.at[pl.ds(first + at * block, block)]
        target = held_ref.at[pl.ds(at * block, block)]
        copies.append(pltpu.make_async_copy(source, target, sems.at[at]))
        copies[-1].start()
    for at in range(count):
        copies[at].wait()

        def plane(z, carry):
            for p in range(per):
                for g in range(2):
                    y = (p * 2 + g) * SUB
                    x = held_ref[at * block : (at + 1) * block, z, y : y + SUB, :]
                    hi, lo = halves(x.reshape(block * SUB, lanes))
                    rows = slice(at * block * SUB, (at + 1) * block * SUB)
                    hi_ref[z * per + p, rows, g * lanes : (g + 1) * lanes] = hi
                    lo_ref[z * per + p, rows, g * lanes : (g + 1) * lanes] = lo
            return carry

        lax.fori_loop(0, planes, plane, 0)


def split(orbitals, first, orbs):
    _, planes, ny, nx = orbitals.shape
    count = orbs // 8 if orbs <= 32 else orbs // 16
    shape = pltpu.VMEM((planes * ny // (2 * SUB), orbs * SUB, 2 * nx), BF16)
    return pl.pallas_call(
        functools.partial(split_kernel, first, count),
        in_specs=[pl.BlockSpec(memory_space=pl.ANY)],
        out_specs=[VMEM, VMEM],
        out_shape=[shape, shape],
        scratch_shapes=[
            pltpu.VMEM((orbs, planes, ny, nx), F32),
            pltpu.SemaphoreType.DMA((count,)),
        ],
        compiler_params=params(),
        name="split",
    )(far_off(orbitals))


def local_kernel(pot_ref, *refs):
    half = len(refs) // 2
    for v_ref, out_ref in zip(refs[:half], refs[half:]):
        cols, planes, _, _ = v_ref.shape

        def column(c, carry):
            for z in range(planes):
                v = v_ref[c, z]
                total = (pot_ref[z] - 1.5 * COEFFS[0]) * v
                for k in range(1, WIDTH + 1):
                    along = pltpu.roll(v, k, 1) + pltpu.roll(v, v.shape[1] - k, 1)
                    along = along + pltpu.roll(v, k, 0) + pltpu.roll(v, v.shape[0] - k, 0)
                    if z + k < planes:
                        along = along + v_ref[c, z + k]
                    if z - k >= 0:
                        along = along + v_ref[c, z - k]
                    total = total - (0.5 * COEFFS[k]) * along
                out_ref[c, z] = total
            return carry

        lax.fori_loop(0, cols, column, 0)


def halo_kernel(side_ref, own_ref, one_ref, two_ref, out_ref):
    cols, planes, _, _ = out_ref.shape

    def fill(before_ref, after_ref):
        def column(c, carry):
            for z in range(planes):
                total = own_ref[c, z]
                for k in range(1, WIDTH + 1):
                    if z - k < 0:
                        total = total - (0.5 * COEFFS[k]) * before_ref[c, planes + z - k]
                    if z + k >= planes:
                        total = total - (0.5 * COEFFS[k]) * after_ref[c, z + k - planes]
                out_ref[c, z] = total
            return carry

        lax.fori_loop(0, cols, column, 0)

    @pl.when(side_ref[0] == 0)
    def _():
        fill(two_ref, one_ref)

    @pl.when(side_ref[0] != 0)
    def _():
        fill(one_ref, two_ref)


def rows_of(refs, z, y):
    return jnp.concatenate(
        [
            jnp.concatenate(
                [
                    ref[:, z, y + g * SUB : y + (g + 1) * SUB, :].reshape(
                        ref.shape[0] * SUB, ref.shape[3]
                    )
                    for ref in refs
                ],
                axis=0,
            )
            for g in range(2)
        ],
        axis=1,
    )


def corr_kernel(parts, count, *refs):
    split_refs, blocks = refs[: 2 * parts], refs[2 * parts : 2 * parts + count]
    out_ref = refs[2 * parts + count]
    big_refs, small_refs = refs[-2 * parts : -parts], refs[-parts:]
    planes, ny = blocks[0].shape[1:3]
    per = ny // (2 * SUB)
    width = sum(b.shape[0] for b in blocks) * SUB
    contract = (((1,), (1,)), ((), ()))
    for p in range(planes * per):
        w_hi, w_lo = halves(rows_of(blocks, p // per, (p % per) * 2 * SUB))
        both = jnp.concatenate([w_hi, w_lo], axis=0)
        for part in range(parts):
            hi_ref, lo_ref = split_refs[2 * part : 2 * part + 2]
            big = lax.dot_general(hi_ref[p], both, contract, preferred_element_type=F32)
            small = lax.dot_general(lo_ref[p], w_hi, contract, preferred_element_type=F32)
            if p == 0:
                big_refs[part][...] = big
                small_refs[part][...] = small
            else:
                big_refs[part][...] += big
                small_refs[part][...] += small
    cols = width // SUB
    pick = lax.broadcasted_iota(jnp.int32, (cols, width), 1) // SUB
    pick = pick == lax.broadcasted_iota(jnp.int32, (cols, width), 0)
    diags = []
    for part in range(parts):
        big_ref = big_refs[part]
        total = big_ref[:, :width] + big_ref[:, width:] + small_refs[part][...]
        total = total.reshape(total.shape[0] // SUB, SUB, width)
        at = lax.broadcasted_iota(jnp.int32, total.shape, 1)
        lane = lax.broadcasted_iota(jnp.int32, total.shape, 2)
        diags.append(jnp.sum(jnp.where(lane % SUB == at, total, 0.0), axis=1))
    out_ref[...] = lax.dot_general(
        pick.astype(F32),
        jnp.concatenate(diags, axis=0),
        contract,
        precision=lax.Precision.HIGHEST,
        preferred_element_type=F32,
    )


def correlate(splits, blocks):
    cols = sum(b.shape[0] for b in blocks)
    rows = [hi.shape[1] for hi, _ in splits]
    parts = len(splits)
    flat = [x for pair in splits for x in pair]
    return pl.pallas_call(
        functools.partial(corr_kernel, parts, len(blocks)),
        in_specs=[VMEM] * (len(flat) + len(blocks)),
        out_specs=VMEM,
        out_shape=pltpu.VMEM((cols, sum(rows) // SUB), F32),
        compiler_params=params(),
        scratch_shapes=[pltpu.VMEM((r, 2 * cols * SUB), F32) for r in rows]
        + [pltpu.VMEM((r, cols * SUB), F32) for r in rows],
        name="corr",
    )(*map(near, flat), *map(near, blocks))


def add_kernel(*refs):
    total = refs[0][...]
    for ref in refs[1:-1]:
        total = total + ref[...]
    refs[-1][...] = total


def add(*parts):
    return pl.pallas_call(
        add_kernel,
        in_specs=[VMEM] * len(parts),
        out_specs=VMEM,
        out_shape=pltpu.VMEM(parts[0].shape, F32),
        compiler_params=params(),
        name="add",
    )(*map(near, parts))


def remove_kernel(planes, parts, splits, keep_ref, send_ref):
    parts = [ref[...] for ref in parts]
    cols, orbs = parts[0].shape
    nx = splits[0].shape[2] // 2
    per = keep_ref.shape[2] // (2 * SUB)
    half = keep_ref.shape[0]
    height = cols * SUB
    corr = parts[0]
    for part in parts[1:]:
        corr = corr + part
    tall = jnp.broadcast_to(corr[:, None, :], (cols, SUB, orbs)).reshape(height, orbs)
    tall = halves(tall)
    tables, held = [], 0
    for hi_ref in splits[::2]:
        rows = hi_ref.shape[1]
        at = lax.broadcasted_iota(jnp.int32, (height, rows), 0) % SUB
        same = at == lax.broadcasted_iota(jnp.int32, (height, rows), 1) % SUB
        spread = lax.broadcasted_iota(jnp.int32, (orbs, rows), 1) // SUB + held
        spread = spread == lax.broadcasted_iota(jnp.int32, (orbs, rows), 0)
        spread = spread.astype(BF16)
        picked = [jnp.dot(x, spread, preferred_element_type=F32) for x in tall]
        picked = [jnp.where(same, x, 0.0).astype(BF16) for x in picked]
        tables.append((jnp.concatenate(picked, axis=0), picked[0]))
        held += rows // SUB
    for z in planes:
        for p in range(per):
            total = None
            for (both, c_hi), hi_ref, lo_ref in zip(tables, splits[::2], splits[1::2]):
                big = jnp.dot(both, hi_ref[z * per + p], preferred_element_type=F32)
                small = jnp.dot(c_hi, lo_ref[z * per + p], preferred_element_type=F32)
                some = big[:height] + big[height:] + small
                total = some if total is None else total + some
            y = p * 2 * SUB
            for g in range(2):
                part = total[:, g * nx : (g + 1) * nx].reshape(cols, SUB, nx)
                rows = slice(y + g * SUB, y + (g + 1) * SUB)
                keep_ref[:, z - planes[0], rows, :] = part[:half]
                send_ref[:, z - planes[0], rows, :] = part[half:]
    return corr


def first_kernel(count, planes, *refs):
    remove_kernel(planes, refs[:count], refs[count:-2], *refs[-2:])


def last_kernel(order, count, planes, me_ref, *refs):
    out_ref = refs[-1]
    corr = remove_kernel(planes, refs[:count], refs[count:-3], *refs[-3:-1])
    step = corr.shape[0] // len(order)
    pieces = [None] * len(order)
    for at, r in enumerate(order):
        pieces[r] = corr[at * step : (at + 1) * step]
    mask = 1
    while mask < len(order):
        swap = (me_ref[0] & mask) != 0
        pieces = [jnp.where(swap, pieces[r ^ mask], pieces[r]) for r in range(len(order))]
        mask *= 2
    out_ref[...] = jnp.concatenate(pieces, axis=0)


def remove(parts, splits, planes, ny, nx, order=None, me=None):
    cols, orbs = parts[0].shape
    part = pltpu.VMEM((cols // 2, len(planes), ny, nx), F32)
    flat = [x for pair in splits for x in pair]
    in_specs = [VMEM] * (len(parts) + len(flat))
    args = [*map(near, parts), *map(near, flat)]
    shape = [part, part]
    kernel = functools.partial(first_kernel, len(parts), planes)
    if order is not None:
        in_specs = [pl.BlockSpec(memory_space=pltpu.SMEM)] + in_specs
        args = [me] + args
        shape = shape + [pltpu.VMEM((cols, orbs), F32)]
        kernel = functools.partial(last_kernel, order, len(parts), planes)
    return pl.pallas_call(
        kernel,
        in_specs=in_specs,
        out_specs=[VMEM] * len(shape),
        out_shape=shape,
        compiler_params=params(),
        name="remove",
    )(*args)


def merge_kernel(keep_ref, got_ref, own_ref, send_ref):
    half = own_ref.shape[0]
    own_ref[...] = keep_ref[:half] + got_ref[:half]
    send_ref[...] = keep_ref[half:] + got_ref[half:]


def merge(keep, got):
    half = pltpu.VMEM((keep.shape[0] // 2,) + keep.shape[1:], F32)
    return pl.pallas_call(
        merge_kernel,
        in_specs=[VMEM] * 2,
        out_specs=[VMEM] * 2,
        out_shape=[half, half],
        compiler_params=params(),
        name="merge",
    )(near(keep), near(got))


def finish_kernel(first, count, *refs):
    blocks, kept_ref, got_ref = refs[:count], refs[count], refs[count + 1]
    out_ref, held_ref, sem = refs[-3:]
    planes = kept_ref.shape[1]
    c = 0
    for block in blocks:
        for at in range(block.shape[0]):
            removed = kept_ref[c] + got_ref[c]
            held_ref[c] = block[at, first : first + planes] - removed
            c += 1
    copy = pltpu.make_async_copy(held_ref, out_ref.at[:, pl.ds(first, planes)], sem)
    copy.start()
    copy.wait()


def finish(first, blocks, kept, got, shape, out=None):
    hbm = pl.BlockSpec(memory_space=pl.ANY)
    args = [*map(near, blocks), near(kept), near(got)]
    in_specs = [VMEM] * len(args)
    aliases = {}
    if out is not None:
        aliases = {len(args): 0}
        args, in_specs = args + [out], in_specs + [hbm]
    return pl.pallas_call(
        functools.partial(finish_kernel, first, len(blocks)),
        in_specs=in_specs,
        out_specs=hbm,
        out_shape=jax.ShapeDtypeStruct(shape, F32),
        input_output_aliases=aliases,
        scratch_shapes=[pltpu.VMEM(kept.shape, F32), pltpu.SemaphoreType.DMA],
        compiler_params=params(),
        name="finish",
    )(*args)


def swap(x, axis, mask):
    size = lax.axis_size(axis)
    return lax.ppermute(x, axis, [(i, i ^ mask) for i in range(size)])


def shards(columns, potential, orbitals):
    cols, planes, ny, nx = columns.shape
    space, band = lax.axis_size("space"), lax.axis_size("band")
    even = [(i, i ^ 1) for i in range(space)]
    odd = [(i, (i + 2 * (i % 2) - 1) % space) for i in range(space)]
    cuts = [0, cols // 2, cols // 2 + cols // 4, cols]
    cuts = [(a, b) for a, b in zip(cuts, cuts[1:]) if b > a]
    side = (lax.axis_index("space") & 1).astype(jnp.int32).reshape(1)
    me = lax.axis_index("band").astype(jnp.int32).reshape(1)
    columns, me, side = lax.optimization_barrier((columns, me, side))
    (*pieces, potential), halos = cut(columns, potential, cuts), []
    for piece in pieces:
        one = lax.ppermute(piece, "space", even)
        halos.append((one, lax.ppermute(piece, "space", odd)))
    splits, held = [], 0
    for share in (3, 1):
        some = orbitals.shape[0] * share // 4
        splits.append(split(orbitals, held, some))
        held += some
    own = pl.pallas_call(
        local_kernel,
        in_specs=[VMEM] * (1 + len(cuts)),
        out_specs=[VMEM] * len(cuts),
        out_shape=[pltpu.VMEM(piece.shape, F32) for piece in pieces],
        compiler_params=params(),
        name="local",
    )(near(potential), *map(near, pieces))

    chunks, order = [], [0]
    for at, (one, two) in enumerate(halos):
        chunk = pl.pallas_call(
            halo_kernel,
            in_specs=[pl.BlockSpec(memory_space=pltpu.SMEM)] + [VMEM] * 3,
            out_specs=VMEM,
            out_shape=pltpu.VMEM(two.shape, F32),
            compiler_params=params(),
            name="halo",
        )(side, near(own[at]), near(one), near(two))
        chunks.append([chunk])
    applied = [c[0] for c in chunks]
    mask = band // 2
    while mask:
        for at, c in enumerate(chunks):
            more = []
            for block in c:
                more.append(swap(block, "band", mask))
            chunks[at] = c + more
        order = order + [r ^ mask for r in order]
        mask //= 2
    blocks = [c[at] for at in range(len(order)) for c in chunks]
    corr = correlate(splits, blocks)
    steps = [[1, 2, 3]] + [[1 << bit] for bit in range(2, space.bit_length() - 1)]
    parts = [corr]
    for step in steps:
        held = parts[0] if len(parts) == 1 else add(*parts)
        parts = [held] + [swap(held, "space", mask) for mask in step]

    low, high = tuple(range(planes // 2)), tuple(range(planes // 2, planes))
    keep0, send0 = remove(parts, splits, low, ny, nx)
    keep1, send1, corr = remove(parts, splits, high, ny, nx, order, me)
    out = None
    kept = [(keep0, send0), (keep1, send1)]
    mask = 1
    while mask < band:
        for at, (keep, send) in enumerate(kept):
            got = swap(send, "band", mask)
            if 2 * mask < band:
                kept[at] = merge(keep, got)
            else:
                first = (low, high)[at][0]
                out = finish(first, applied, keep, got, columns.shape, out)
        mask *= 2
    return out, corr.T


def solution(mesh):
    placed = (
        P("band", "space", None, None),
        P("space", None, None),
        P("band", "space", None, None),
    )

    return jax.shard_map(
        shards,
        mesh=mesh,
        in_specs=placed,
        out_specs=(P("band", "space", None, None), P("band", None)),
        check_vma=False,
    )
```
